128 devices in a mesh: expert: 32 (over z, x, core), replica: 4 (over y).
Axes of the slice: x: 4, y: 4, z: 4, core: 2. Of those that a mesh axis runs over, the one named last changes fastest.
Arguments:
- x_tokens: bfloat16 [16384, 2048], P(('expert', 'replica')), may hold values from -6 to 6
- d_out: bfloat16 [16384, 2048], P(('expert', 'replica')), may hold values from -3 to 3
- expert_ids: int32 [16384, 2], P(('expert', 'replica')), may hold values from 0 to 31, all different within a row; in each aligned block of 128 rows (0 to 127, 128 to 255, ...) at most 16 rows name the same one
- combine: float32 [16384, 2], P(('expert', 'replica')), may hold values from 0.1 to 1
- w_stack: bfloat16 [32, 1408, 6144], P('expert'), may hold values from -0.125 to 0.125
Outputs:
- d_tokens: bfloat16 [16384, 2048], P(('expert', 'replica'))
- g_stack: bfloat16 [32, 1408, 6144], P('expert', 'replica')
The draws below stay inside these ranges and needn't reach their ends.
Inputs may be any that keep to these rules, and one draw needn't show every extreme that they name: `expert_ids`: in the tokens of one device (aligned blocks of 128 tokens) each expert is named by at most 16 routes, and by exactly 16 in some block; a token's 2 experts differ.
All inputs are finite; a program needn't handle non-finite values.
Results may differ from the reference program's by a relative error of at most 0.013.
Values may be sent and summed in bfloat16 or wider, within the bound.
A program may use at most 128 MiB of HBM per device.

```python
import math
import jax
import jax.numpy as jnp
import numpy as np
from jax import lax

D = 2048
FF = 1408
TOK_DEV = 128
TOPW = 2
EXPERTS = 32
CAP = 16
TOKENS = 16384
N_EXPERT = 32
N_REPLICA = 4


def block_scale(key, shape, cuts, least, top_value):
    gain = 1.0
    for position, blocks in cuts:
        steps = jax.random.uniform(jax.random.fold_in(jax.random.fold_in(key, 6), position), (blocks,), jnp.float32, least / len(cuts), top_value / len(cuts))
        gain = gain * jnp.repeat(jnp.exp(steps), shape[position] // blocks).reshape((-1,) + (1,) * (len(shape) - 1 - position))
    return gain


def assign_block(own_key, own, number, rows, amount, top, limit, slope):
    sequence = jax.random.permutation(own_key, amount)
    crowded, common = portions_of(amount, rows * top, limit, slope, True), portions_of(amount, rows * top, limit, slope, False)
    places = jnp.arange(amount)

    def named(tallies, rotation):
        used = int((tallies > 0).sum())
        fixed = max(1, used // 4)
        shifted = fixed + (places - fixed + rotation * (used - fixed)) % max(1, amount - fixed)
        return jnp.zeros((amount,), jnp.int32).at[sequence[jnp.where(places < fixed, places, shifted)]].set(jnp.asarray(tallies, jnp.int32))

    tallies = jnp.where(number % 4 == 0, named(crowded, number // 4), named(common, number - number // 4 - 1))
    mixed = jax.random.permutation(jax.random.fold_in(own, 3), amount)
    source_of, taker = mixed[0:amount // 2 * 2:2], mixed[1:amount // 2 * 2:2]
    room = jnp.minimum(tallies[source_of] - 1, limit - tallies[taker]) // 2
    room = jnp.where((source_of == sequence[0]) | (taker == sequence[0]) | (tallies[taker] == 0), 0, jnp.maximum(room, 0))
    shifted = jax.random.randint(jax.random.fold_in(own, 4), (amount // 2,), 0, 1 << 20) % (room + 1)
    tallies = tallies.at[source_of].add(-shifted).at[taker].add(shifted)
    items = jnp.searchsorted(jnp.cumsum(tallies), jnp.arange(rows * top), side="right").astype(jnp.int32)
    table = items.reshape(top, rows).T
    table = table[jax.random.permutation(jax.random.fold_in(own, 1), rows)]
    rotation = jax.random.randint(jax.random.fold_in(own, 2), (rows, 1), 0, top)
    return jnp.take_along_axis(table, (jnp.arange(top)[None, :] + rotation) % top, axis=1)


def portions_of(count, total, bound, lean, full):
    weights = [(1 << 20) // math.isqrt(standing ** lean) + 1 for standing in range(1, count + 1)]
    largest = bound if full else min(bound, max(-(-total // count), total * weights[0] // sum(weights)))
    least = 1 if total - largest >= count - 1 else 0
    holding, surplus = [largest] + [least] * (count - 1), total - largest - least * (count - 1)
    while surplus > 0:
        movable = [i for i in range(1, count) if holding[i] < largest] or [i for i in range(1, count) if holding[i] < bound]
        whole, budget = sum([weights[i] for i in movable]), surplus
        for i in movable:
            extra = min(bound - holding[i], max(1, budget * weights[i] // whole), surplus)
            holding[i] = holding[i] + extra
            surplus = surplus - extra
    return np.array(holding)


def noise(own_key, shape, spread, most, shards=(), kind=jnp.bfloat16):
    drawn = jax.random.normal(own_key, shape, jnp.float32) * spread
    if len(shards) > 0:
        drawn = block_scale(own_key, shape, shards, -0.22, 0.18) * drawn
    return jnp.clip(drawn, min=-most, max=most).astype(kind)


def setup_inputs(seed: int = 0) -> dict:
    seeds = jax.random.split(jax.random.key(seed), 6)
    x_tokens = noise(seeds[0], (TOKENS, D), 1.0, 6.0, ((0, 128),))
    d_out = noise(seeds[1], (TOKENS, D), 0.5, 3.0, ((0, 128),))
    expert_ids_keys = jax.random.split(jax.random.fold_in(seeds[2], 1), TOKENS // TOK_DEV)
    expert_ids_turns = jax.random.permutation(jax.random.fold_in(seeds[2], 3), TOKENS // TOK_DEV)
    expert_ids = jax.vmap(lambda own, number: assign_block(jax.random.fold_in(seeds[2], 2), own, number, TOK_DEV, EXPERTS, TOPW, CAP, 2))(expert_ids_keys, expert_ids_turns).reshape((TOKENS, TOPW))
    combine = jnp.clip(jnp.exp(math.log(1.0) - 2.3025851 * jax.random.uniform(seeds[3], (TOKENS, TOPW), jnp.float32) ** block_scale(seeds[3], (TOKENS, TOPW), ((0, 128),), -0.2, 0.2)), 0.1, 1.0)
    w_stack = noise(seeds[4], (EXPERTS, FF, 3 * D), D ** -0.5, 0.125, ((0, 32),))
    return {"x_tokens": x_tokens, "d_out": d_out, "expert_ids": expert_ids, "combine": combine, "w_stack": w_stack}


def reference(x_tokens, d_out, expert_ids, combine, w_stack):
    block_count = N_EXPERT * N_REPLICA
    route_count = TOK_DEV * TOPW
    slot_total = N_EXPERT * CAP
    route_ids = expert_ids.reshape(block_count, route_count)
    member = (route_ids[:, :, None] == jnp.arange(EXPERTS, dtype=jnp.int32)[None, None, :]).astype(jnp.int32)
    slot_rank = jnp.sum((jnp.cumsum(member, axis=1) - 1) * member, axis=2).astype(jnp.int32)
    block_index = jnp.arange(block_count, dtype=jnp.int32)[:, None]
    slot_target = ((route_ids * block_count + block_index) * CAP + slot_rank).astype(jnp.int32)
    slot_table = jnp.full((EXPERTS * block_count * CAP,), -1, jnp.int32)
    slot_table = slot_table.at[slot_target.reshape(-1)].set(jnp.arange(block_count * route_count, dtype=jnp.int32))
    slot_table = slot_table.reshape(EXPERTS, N_EXPERT, N_REPLICA, CAP).transpose(0, 2, 1, 3)
    slot_table = slot_table.reshape(EXPERTS, N_REPLICA * slot_total)
    dy_routes = (combine.reshape(-1, 1) * jnp.repeat(d_out, TOPW, axis=0).astype(jnp.float32)).astype(jnp.bfloat16)
    x_routes = jnp.repeat(x_tokens, TOPW, axis=0)

    def one_expert(dx_total, inputs):
        routes, weights = inputs
        is_valid = routes >= 0
        route_index = jnp.maximum(routes, 0).astype(jnp.int32)
        row_block = jnp.where(is_valid[:, None], x_routes[route_index], jnp.zeros((), jnp.bfloat16))
        grads_in = jnp.where(is_valid[:, None], dy_routes[route_index], jnp.zeros((), jnp.bfloat16))
        w_gate = weights[:, :D]
        w_up = weights[:, D:2 * D]
        w_down = weights[:, 2 * D:]
        gate_pre = jnp.dot(row_block, w_gate.T, preferred_element_type=jnp.float32)
        up_pre = jnp.dot(row_block, w_up.T, preferred_element_type=jnp.float32)
        d_hidden = jnp.dot(grads_in, w_down.T, preferred_element_type=jnp.float32)
        gate_sigmoid = jax.nn.sigmoid(gate_pre)
        gate_act = gate_pre * gate_sigmoid
        hidden_act = (gate_act * up_pre).astype(jnp.bfloat16)
        d_up = (d_hidden * gate_act).astype(jnp.bfloat16)
        d_gate = (d_hidden * up_pre * gate_sigmoid * (1.0 + gate_pre * (1.0 - gate_sigmoid))).astype(jnp.bfloat16)
        dx_rows = jnp.dot(d_gate, w_gate, preferred_element_type=jnp.float32) + jnp.dot(d_up, w_up, preferred_element_type=jnp.float32)
        dx_rows = jnp.where(is_valid[:, None], dx_rows, jnp.zeros((), jnp.float32))
        dx_total = dx_total.at[route_index].add(dx_rows)
        x_groups = row_block.reshape(N_REPLICA, slot_total, D).astype(jnp.float32)
        dy_groups = grads_in.reshape(N_REPLICA, slot_total, D).astype(jnp.float32)
        gate_groups = d_gate.reshape(N_REPLICA, slot_total, FF).astype(jnp.float32)
        up_groups = d_up.reshape(N_REPLICA, slot_total, FF).astype(jnp.float32)
        act_groups = hidden_act.reshape(N_REPLICA, slot_total, FF).astype(jnp.float32)
        partial_value = jnp.concatenate([
            jnp.einsum("grj,grd->gjd", gate_groups, x_groups),
            jnp.einsum("grj,grd->gjd", up_groups, x_groups),
            jnp.einsum("grj,grd->gjd", act_groups, dy_groups)], axis=2)
        rounded = lax.optimization_barrier(partial_value.astype(jnp.bfloat16)).astype(jnp.float32)
        grad_stack = jnp.sum(rounded, axis=0).astype(jnp.bfloat16)
        return dx_total, grad_stack

    dx_start = jnp.zeros((TOKENS * TOPW, D), jnp.float32)
    dx_all, g_stack = lax.scan(one_expert, dx_start, (slot_table, w_stack))
    d_tokens = jnp.sum(dx_all.reshape(TOKENS, TOPW, D), axis=1).astype(jnp.bfloat16)
    return d_tokens, g_stack
```

```python
import functools

import jax
import jax.numpy as jnp
from jax import lax
from jax.experimental import pallas as pl
from jax.experimental.pallas import tpu as pltpu
from jax.sharding import PartitionSpec as P

MESH = pl.DeviceIdType.MESH
PARTS = 4
OFFSETS = [
    (2, 2), (1, 1), (3, 3), (1, 3), (3, 1), (2, 1), (1, 2), (2, 3),
    (3, 2), (2, 0), (0, 2), (1, 0), (0, 1), (3, 0), (0, 3), (0, 0),
]


def step_of(expert, group):
    return 1 - 2 * ((group + expert) % 2)


def dispatch_kernel(peers, groups, send_ref, own_ref, mate_ref, send_sem, recv_sem, keep_sem, pass_sem, take_sem):
    e = lax.axis_index("expert")
    r = lax.axis_index("replica")
    mate = lax.rem(r + groups + step_of(e, r), groups)
    arrays, width = send_ref.shape[0], send_ref.shape[-1] // PARTS
    total = arrays * PARTS

    barrier = pltpu.get_barrier_semaphore()
    for k in range(1, peers):
        pl.semaphore_signal(barrier, inc=1, device_id=((e + k) % peers, r), device_id_type=MESH)
    pl.semaphore_signal(barrier, inc=1, device_id=(e, mate), device_id_type=MESH)
    pl.semaphore_wait(barrier, peers)

    z, x, c = e // 8, (e // 2) % 4, e % 2
    order = [
        ((z + dz) % 4) * 8 + ((x + dx) % 4) * 2 + (c + dc) % 2
        for dz, dx in OFFSETS
        for dc in (0, 1)
        if (dz, dx, dc) != (0, 0, 0)
    ]

    def place(k):
        return k // PARTS, pl.ds((k % PARTS) * width, width)

    def keep(k):
        a, cols = place(k)
        return pltpu.make_async_copy(send_ref.at[a, e, :, cols], own_ref.at[a, e, :, cols], keep_sem.at[k])

    def remote(k, src, dst, send, recv, device):
        return pltpu.make_async_remote_copy(
            src_ref=src, dst_ref=dst, send_sem=send.at[k], recv_sem=recv.at[k], device_id=device, device_id_type=MESH
        )

    def everyone(k):
        a, cols = place(k)
        some = pl.ds(0, peers - 1)
        return remote(k, send_ref.at[a, some, :, cols], own_ref.at[a, some, :, cols], send_sem, recv_sem, (e, mate))

    def across(k):
        a, cols = place(k)
        return remote(k, own_ref.at[a, :, :, cols], mate_ref.at[a, :, :, cols], pass_sem, take_sem, (e, mate))

    for k in range(total + 1):
        if k < total:
            a, cols = place(k)
            for to in order:
                remote(k, send_ref.at[a, to, :, cols], own_ref.at[a, e, :, cols], send_sem, recv_sem, (to, r)).start()
            keep(k).start()
        if k > 0:
            everyone(k - 1).wait_recv()
            keep(k - 1).wait()
            across(k - 1).start()
    for k in range(total):
        everyone(k).wait_send()
        across(k).wait()


def dispatch(send, groups):
    shape = jax.ShapeDtypeStruct(send.shape, send.dtype)
    return pl.pallas_call(
        functools.partial(dispatch_kernel, send.shape[1], groups),
        out_shape=(shape, shape),
        in_specs=[pl.BlockSpec(memory_space=pltpu.VMEM)],
        out_specs=(pl.BlockSpec(memory_space=pl.ANY),) * 2,
        scratch_shapes=[pltpu.SemaphoreType.DMA((send.shape[0] * PARTS,))] * 5,
        compiler_params=pltpu.CompilerParams(
            collective_id=0, has_side_effects=True, vmem_limit_bytes=40 * 1024 * 1024
        ),
        name="dispatch",
    )(send)


def rows_by_rows(left, right):
    return lax.dot_general(left, right, (((1,), (1,)), ((), ())), preferred_element_type=jnp.float32)


def forward(weights, x, dy, width):
    gate = rows_by_rows(weights[:, :width], x)
    up = rows_by_rows(weights[:, width : 2 * width], x)
    d_hidden = rows_by_rows(weights[:, 2 * width :], dy)
    s = jax.nn.sigmoid(gate)
    act = gate * s
    hidden = (act * up).astype(jnp.bfloat16)
    d_up = (d_hidden * act).astype(jnp.bfloat16)
    d_gate = (d_hidden * up * s * (1.0 + gate * (1.0 - s))).astype(jnp.bfloat16)
    return hidden, d_gate, d_up


def weight_grad(acts, x, dy):
    hidden, d_gate, d_up = acts
    dot = functools.partial(jnp.dot, preferred_element_type=jnp.float32)
    return jnp.concatenate([dot(d_gate, x), dot(d_up, x), dot(hidden, dy)], axis=1)


def body(x_tokens, d_out, expert_ids, combine, w_stack):
    tokens, width = x_tokens.shape
    experts, groups = lax.axis_size("expert"), lax.axis_size("replica")
    capacity = 2 * tokens * expert_ids.shape[1] // experts
    slots = experts * capacity
    e, r = lax.axis_index("expert"), lax.axis_index("replica")
    other = (r + groups - step_of(e, r)) % groups

    ids = expert_ids.T
    iota = jnp.arange(experts, dtype=jnp.int32)
    member = [(ids[k][:, None] == iota[None, :]).astype(jnp.float32) for k in range(ids.shape[0])]
    both = functools.reduce(jnp.add, member)
    lower = (jnp.arange(tokens)[:, None] > jnp.arange(tokens)[None, :]).astype(jnp.float32)
    before = jnp.dot(lower, both, preferred_element_type=jnp.float32)
    slot = jnp.stack(
        [ids[k] * capacity + jnp.sum(before * member[k], axis=1).astype(jnp.int32) for k in range(ids.shape[0])]
    )
    places = [jnp.arange(slots, dtype=jnp.int32)[:, None] == slot[k][None, :] for k in range(ids.shape[0])]
    place = functools.reduce(jnp.logical_or, places).astype(jnp.bfloat16)
    scale = sum(jnp.sum(jnp.where(places[k], combine[:, k][None, :], 0.0), axis=1) for k in range(ids.shape[0]))
    send_x = jnp.dot(place, x_tokens, preferred_element_type=jnp.float32).astype(jnp.bfloat16)
    send_dy = (scale[:, None] * jnp.dot(place, d_out, preferred_element_type=jnp.float32)).astype(jnp.bfloat16)
    send = jnp.stack([send_x, send_dy]).reshape(2, experts, capacity, width)

    own, mate = dispatch(send, groups)
    own, mate = own.reshape(2, slots, width), mate.reshape(2, slots, width)
    weights = w_stack[0]
    hidden = weights.shape[0]
    shard = hidden // groups

    w_other = lax.dynamic_slice_in_dim(weights, other * shard, shard, 0)
    w_mine = lax.dynamic_slice_in_dim(weights, r * shard, shard, 0)

    def both_planes(w):
        a, b = forward(w, own[0], own[1], width), forward(w, mate[0], mate[1], width)
        ga, gb = weight_grad(a, own[0], own[1]), weight_grad(b, mate[0], mate[1])
        return ga + gb

    pairs = []
    for i in range(experts):
        for g in range(groups):
            pairs.append((i * groups + g, i * groups + (g - step_of(i, g)) % groups))
    partial = both_planes(w_other).astype(jnp.bfloat16)
    theirs = lax.ppermute(partial, ("expert", "replica"), pairs)
    own, mate, partial = lax.optimization_barrier((own, mate, partial))

    _, d_gate, d_up = forward(weights, own[0], own[1], width)
    rows = (((0,), (0,)), ((), ()))
    dx = lax.dot_general(d_gate, weights[:, :width], rows, preferred_element_type=jnp.float32) + lax.dot_general(
        d_up, weights[:, width : 2 * width], rows, preferred_element_type=jnp.float32
    )
    dx = dx.astype(jnp.bfloat16)
    own, mate, dx = lax.optimization_barrier((own, mate, dx))
    back = lax.all_to_all(
        dx.reshape(experts, capacity, width), "expert", split_axis=0, concat_axis=0, tiled=True
    )
    d_tokens = lax.dot_general(
        place, back.reshape(slots, width), rows, preferred_element_type=jnp.float32
    ).astype(jnp.bfloat16)

    mine = both_planes(w_mine)
    g_stack = (mine + theirs.astype(jnp.float32)).astype(jnp.bfloat16)
    return d_tokens, g_stack[None]


def solution(mesh):
    rows = P(("expert", "replica"), None)
    return jax.shard_map(
        body,
        mesh=mesh,
        in_specs=(rows, rows, rows, rows, P("expert", None, None)),
        out_specs=(rows, P("expert", "replica", None)),
        check_vma=False,
    )
```

```python
import functools

import jax
import jax.numpy as jnp
from jax import lax
from jax.experimental import pallas as pl
from jax.experimental.pallas import tpu as pltpu
from jax.sharding import PartitionSpec as P

MESH = pl.DeviceIdType.MESH
PARTS = 4
OFFSETS = [
    (2, 2), (1, 1), (3, 3), (1, 3), (3, 1), (2, 1), (1, 2), (2, 3),
    (3, 2), (2, 0), (0, 2), (1, 0), (0, 1), (3, 0), (0, 3), (0, 0),
]


def step_of(expert, group):
    return 1 - 2 * ((group + expert) % 2)


def dispatch_kernel(peers, groups, send_ref, own_ref, mate_ref, send_sem, recv_sem, keep_sem, pass_sem, take_sem):
    e = lax.axis_index("expert")
    r = lax.axis_index("replica")
    mate = lax.rem(r + groups + step_of(e, r), groups)
    arrays, width = send_ref.shape[0], send_ref.shape[-1] // PARTS
    total = arrays * PARTS

    barrier = pltpu.get_barrier_semaphore()
    for k in range(1, peers):
        pl.semaphore_signal(barrier, inc=1, device_id=((e + k) % peers, r), device_id_type=MESH)
    pl.semaphore_signal(barrier, inc=1, device_id=(e, mate), device_id_type=MESH)
    pl.semaphore_wait(barrier, peers)

    z, x, c = e // 8, (e // 2) % 4, e % 2
    order = [
        ((z + dz) % 4) * 8 + ((x + dx) % 4) * 2 + (c + dc) % 2
        for dz, dx in OFFSETS
        for dc in (0, 1)
        if (dz, dx, dc) != (0, 0, 0)
    ]

    def place(k):
        return k // PARTS, pl.ds((k % PARTS) * width, width)

    def keep(k):
        a, cols = place(k)
        return pltpu.make_async_copy(send_ref.at[a, e, :, cols], own_ref.at[a, e, :, cols], keep_sem.at[k])

    def remote(k, src, dst, send, recv, device):
        return pltpu.make_async_remote_copy(
            src_ref=src, dst_ref=dst, send_sem=send.at[k], recv_sem=recv.at[k], device_id=device, device_id_type=MESH
        )

    def everyone(k):
        a, cols = place(k)
        some = pl.ds(0, peers - 1)
        return remote(k, send_ref.at[a, some, :, cols], own_ref.at[a, some, :, cols], send_sem, recv_sem, (e, mate))

    def across(k):
        a, cols = place(k)
        return remote(k, own_ref.at[a, :, :, cols], mate_ref.at[a, :, :, cols], pass_sem, take_sem, (e, mate))

    for k in range(total + 1):
        if k < total:
            a, cols = place(k)
            for to in order:
                remote(k, send_ref.at[a, to, :, cols], own_ref.at[a, e, :, cols], send_sem, recv_sem, (to, r)).start()
            keep(k).start()
        if k > 0:
            everyone(k - 1).wait_recv()
            keep(k - 1).wait()
            across(k - 1).start()
    for k in range(total):
        everyone(k).wait_send()
        across(k).wait()


def dispatch(send, groups):
    shape = jax.ShapeDtypeStruct(send.shape, send.dtype)
    return pl.pallas_call(
        functools.partial(dispatch_kernel, send.shape[1], groups),
        out_shape=(shape, shape),
        in_specs=[pl.BlockSpec(memory_space=pltpu.VMEM)],
        out_specs=(pl.BlockSpec(memory_space=pl.ANY),) * 2,
        scratch_shapes=[pltpu.SemaphoreType.DMA((send.shape[0] * PARTS,))] * 5,
        compiler_params=pltpu.CompilerParams(
            collective_id=0, has_side_effects=True, vmem_limit_bytes=40 * 1024 * 1024
        ),
        name="dispatch",
    )(send)


def expert_kernel(
    peers, groups, own_ref, mate_ref, w_ref, back_ref, g_ref,
    rows, weights, acts, turned, grad_in, partial, theirs,
    row_sem, w_sem, bar_send, bar_recv, dx_send, dx_recv, keep_sem,
):
    e = lax.axis_index("expert")
    r = lax.axis_index("replica")
    step = step_of(e, r)
    other = lax.rem(r + groups - step, groups)
    held, width = own_ref.shape[1], own_ref.shape[2]
    hidden = w_ref.shape[0]
    shard = hidden // groups
    chunk = partial.shape[2]
    chunks = partial.shape[0]
    per = width // chunk
    cap = held // peers
    f32, bf16 = jnp.float32, jnp.bfloat16

    barrier = pltpu.get_barrier_semaphore()
    for k in range(1, peers):
        pl.semaphore_signal(barrier, inc=1, device_id=((e + k) % peers, r), device_id_type=MESH)
    pl.semaphore_signal(barrier, inc=1, device_id=(e, other), device_id_type=MESH)

    shards = [other, r, lax.rem(r + groups + step, groups), lax.rem(r + 2, groups)]
    loads = [
        pltpu.make_async_copy(
            w_ref.at[pl.ds(pl.multiple_of(at * shard, 32), shard), :],
            weights.at[pl.ds(i * shard, shard), :],
            w_sem.at[i],
        )
        for i, at in enumerate(shards)
    ]
    takes = [
        pltpu.make_async_copy(ref.at[a], rows.at[a, pl.ds(p * held, held), :], row_sem.at[a, p])
        for a in (0, 1)
        for p, ref in enumerate((own_ref, mate_ref))
    ]
    for copy in loads[:1] + takes + loads[1:]:
        copy.start()

    def forward(i, first, count):
        span = 256
        ws = pl.ds(i * shard, shard)

        def tile(t, _):
            at = pl.ds(pl.multiple_of(first + t * span, span), span)
            dims = (((1,), (1,)), ((), ()))
            gate = lax.dot_general(weights[ws, 0:width], rows[0, at, :], dims, preferred_element_type=f32)
            up = lax.dot_general(weights[ws, width : 2 * width], rows[0, at, :], dims, preferred_element_type=f32)
            d_hidden = lax.dot_general(
                weights[ws, 2 * width : 3 * width], rows[1, at, :], dims, preferred_element_type=f32
            )
            s = jax.nn.sigmoid(gate)
            act = gate * s
            acts[0, ws, at] = (d_hidden * up * s * (1.0 + gate * (1.0 - s))).astype(bf16)
            acts[1, ws, at] = (d_hidden * act).astype(bf16)
            acts[2, ws, at] = (act * up).astype(bf16)
            return 0

        lax.fori_loop(0, count // span, tile, 0)

    def weight_grad(i, j):
        part = j // per
        cols = pl.ds(pl.multiple_of(lax.rem(j, per) * chunk, chunk), chunk)
        return jnp.dot(
            acts[part, pl.ds(i * shard, shard), :], rows[part // 2, :, cols], preferred_element_type=f32
        )

    def send_partial(j):
        return pltpu.make_async_remote_copy(
            src_ref=partial.at[j], dst_ref=theirs.at[j], send_sem=bar_send.at[j], recv_sem=bar_recv.at[j],
            device_id=(e, other), device_id_type=MESH,
        )

    z, x, c = e // 8, (e // 2) % 4, e % 2
    order = [
        ((z + dz) % 4) * 8 + ((x + dx) % 4) * 2 + (c + dc) % 2
        for dz, dx in OFFSETS
        for dc in (0, 1)
        if (dz, dx, dc) != (0, 0, 0)
    ]
    halves = 2
    half = width // halves

    def send_rows(h, to):
        cols = pl.ds(h * half, half)
        return pltpu.make_async_remote_copy(
            src_ref=grad_in.at[to, :, cols], dst_ref=back_ref.at[e, :, cols], send_sem=dx_send.at[h],
            recv_sem=dx_recv.at[h], device_id=(to, r), device_id_type=MESH,
        )

    def all_rows(h):
        cols = pl.ds(h * half, half)
        some = pl.ds(0, peers - 1)
        return pltpu.make_async_remote_copy(
            src_ref=grad_in.at[some, :, cols], dst_ref=back_ref.at[some, :, cols], send_sem=dx_send.at[h],
            recv_sem=dx_recv.at[h], device_id=(e, other), device_id_type=MESH,
        )

    def keep(h):
        cols = pl.ds(h * half, half)
        return pltpu.make_async_copy(grad_in.at[e, :, cols], back_ref.at[e, :, cols], keep_sem.at[h])

    for copy in loads[:1] + takes:
        copy.wait()
    forward(0, 0, 2 * held)
    pl.semaphore_wait(barrier, peers)

    def first_pass(j, _):
        partial[j] = weight_grad(0, j).astype(bf16)

        @pl.when(j > 0)
        def _():
            send_partial(j - 1).start()

        return 0

    lax.fori_loop(0, chunks, first_pass, 0)
    for copy in loads[1:]:
        copy.wait()
    send_partial(chunks - 1).start()
    for i in range(1, groups):
        forward(i, 0, held)

    def turn(t, _):
        at = pl.ds(pl.multiple_of(t * 128, 128), 128)
        for part in (0, 1):
            turned[part, at, :] = jnp.transpose(acts[part, :, at])
        return 0

    lax.fori_loop(0, held // 128, turn, 0)

    for h in range(halves):

        def columns(t, _):
            at = pl.multiple_of(h * half + t * chunk, chunk)
            total = jnp.dot(turned[0], weights[:, pl.ds(at, chunk)], preferred_element_type=f32)
            total += jnp.dot(turned[1], weights[:, pl.ds(width + at, chunk)], preferred_element_type=f32)
            grad_in[:, :, pl.ds(at, chunk)] = total.astype(bf16).reshape(peers, cap, chunk)
            return 0

        lax.fori_loop(0, half // chunk, columns, 0)
        for to in order:
            send_rows(h, to).start()
        keep(h).start()

    forward(1, held, held)

    def second_pass(j, _):
        mine = weight_grad(1, j)
        send_partial(j).wait_recv()
        g_ref[:, pl.ds(pl.multiple_of(j * chunk, chunk), chunk)] = (mine + theirs[j].astype(f32)).astype(bf16)
        return 0

    lax.fori_loop(0, chunks, second_pass, 0)
    for h in range(halves):
        all_rows(h).wait()
        keep(h).wait()

    def drain(j, _):
        send_partial(j).wait_send()
        return 0

    lax.fori_loop(0, chunks, drain, 0)


def expert_backward(own, mate, weights, peers, groups):
    held, width = own.shape[1:]
    hidden = weights.shape[0]
    shard, chunk = hidden // groups, 512
    chunks = 3 * width // chunk
    anywhere = pl.BlockSpec(memory_space=pl.ANY)
    bf16 = own.dtype
    return pl.pallas_call(
        functools.partial(expert_kernel, peers, groups),
        out_shape=(
            jax.ShapeDtypeStruct((peers, held // peers, width), bf16),
            jax.ShapeDtypeStruct((shard, 3 * width), bf16),
        ),
        in_specs=[anywhere] * 3,
        out_specs=(anywhere, pl.BlockSpec(memory_space=pltpu.VMEM)),
        scratch_shapes=[
            pltpu.VMEM((2, 2 * held, width), bf16),
            pltpu.VMEM((hidden, 3 * width), bf16),
            pltpu.VMEM((3, hidden, 2 * held), bf16),
            pltpu.VMEM((2, held, hidden), bf16),
            pltpu.VMEM((peers, held // peers, width), bf16),
            pltpu.VMEM((chunks, shard, chunk), bf16),
            pltpu.VMEM((chunks, shard, chunk), bf16),
            pltpu.SemaphoreType.DMA((2, 2)),
            pltpu.SemaphoreType.DMA((groups,)),
            pltpu.SemaphoreType.DMA((chunks,)),
            pltpu.SemaphoreType.DMA((chunks,)),
            pltpu.SemaphoreType.DMA((2,)),
            pltpu.SemaphoreType.DMA((2,)),
            pltpu.SemaphoreType.DMA((2,)),
        ],
        compiler_params=pltpu.CompilerParams(
            collective_id=1, has_side_effects=True, vmem_limit_bytes=62 * 1024 * 1024
        ),
        name="expert_backward",
    )(own, mate, weights)


def body(x_tokens, d_out, expert_ids, combine, w_stack):
    tokens, width = x_tokens.shape
    experts, groups = lax.axis_size("expert"), lax.axis_size("replica")
    capacity = 2 * tokens * expert_ids.shape[1] // experts
    slots = experts * capacity

    ids = expert_ids.T
    iota = jnp.arange(experts, dtype=jnp.int32)
    member = [(ids[k][:, None] == iota[None, :]).astype(jnp.float32) for k in range(ids.shape[0])]
    both = functools.reduce(jnp.add, member)
    lower = (jnp.arange(tokens)[:, None] > jnp.arange(tokens)[None, :]).astype(jnp.float32)
    before = jnp.dot(lower, both, preferred_element_type=jnp.float32)
    slot = jnp.stack(
        [ids[k] * capacity + jnp.sum(before * member[k], axis=1).astype(jnp.int32) for k in range(ids.shape[0])]
    )
    places = [jnp.arange(slots, dtype=jnp.int32)[:, None] == slot[k][None, :] for k in range(ids.shape[0])]
    place = functools.reduce(jnp.logical_or, places).astype(jnp.bfloat16)
    scale = sum(jnp.sum(jnp.where(places[k], combine[:, k][None, :], 0.0), axis=1) for k in range(ids.shape[0]))
    send_x = jnp.dot(place, x_tokens, preferred_element_type=jnp.float32).astype(jnp.bfloat16)
    send_dy = (scale[:, None] * jnp.dot(place, d_out, preferred_element_type=jnp.float32)).astype(jnp.bfloat16)
    send = jnp.stack([send_x, send_dy]).reshape(2, experts, capacity, width)

    own, mate = dispatch(send, groups)
    own, mate = own.reshape(2, slots, width), mate.reshape(2, slots, width)
    back, g_shard = expert_backward(own, mate, w_stack[0], experts, groups)
    d_tokens = lax.dot_general(
        place, back.reshape(slots, width), (((0,), (0,)), ((), ())), preferred_element_type=jnp.float32
    ).astype(jnp.bfloat16)
    return d_tokens, g_shard[None]


def solution(mesh):
    rows = P(("expert", "replica"), None)
    return jax.shard_map(
        body,
        mesh=mesh,
        in_specs=(rows, rows, rows, rows, P("expert", None, None)),
        out_specs=(rows, P("expert", "replica", None)),
        check_vma=False,
    )
```
